32 devices in a mesh: ctx: 8 (over z, x), head: 4 (over y, core).
Axes of the slice: x: 2, y: 2, z: 4, core: 2. Of those that a mesh axis runs over, the one named last changes fastest.
Arguments:
- hidden: bfloat16 [8192, 1536], P('ctx', 'head'), may hold values from -6 to 6
- norm_gain: float32 [1536], replicated, may hold values from 0.1 to 1.9
- zx_weight: bfloat16 [1536, 2, 3072], P(None, None, 'head'), may hold values from -0.15625 to 0.15625
- bc_weight: bfloat16 [1536, 256], replicated, may hold values from -0.15625 to 0.15625
- dt_weight: bfloat16 [1536, 48], P(None, 'head'), may hold values from -0.15625 to 0.15625
- conv_x: float32 [5, 3072], P(None, 'head'), may hold values from -0.5 to 0.5
- conv_bc: float32 [5, 256], replicated, may hold values from -0.5 to 0.5
- dt_bias: float32 [48], P('head'), may hold values from -4.6 to -2.3
- log_decay: float32 [8192, 48], P('ctx', 'head'), may hold values from -1.5 to 0, as said below
- skip_gain: float32 [48], P('head'), may hold values from 0.5 to 2
- out_gain: float32 [3072], P('head'), may hold values from 0.1 to 1.9
- out_weight: bfloat16 [3072, 1536], P('head'), may hold values from -0.109375 to 0.109375
Outputs:
- mixed: bfloat16 [8192, 1536], P('ctx', 'head')
The draws below stay inside these ranges and needn't reach their ends.
Inputs may be any that keep to these rules, and one draw needn't show every extreme that they name: `log_decay`: negative everywhere; in some heads a token keeps only a few percent of the state after a few tens of positions, other heads decay over the whole document, and a head may lose a sizeable share of its state at single tokens.
All inputs are finite; a program needn't handle non-finite values.
Results may differ from the reference program's by a relative error of at most 0.015.
Values may be sent and summed in bfloat16 or wider, within the bound.
A program may use at most 128 MiB of HBM per device.

```python
import math
import jax
import jax.numpy as jnp
from jax import lax

D = 1536
HEAD_TOTAL = 48
HEADDIM = 64
STATE = 128
CONV = 4
BLOCK = 256
TOK_DEV = 1024
INNER = 3072
DOCUMENT_LENGTH = 8192
N_HEAD = 4


def draw_log_decay(key, part):
    random_subkeys = jax.random.split(key, 7)
    fast_share = 0.5
    is_fast = jax.random.uniform(random_subkeys[0], (HEAD_TOTAL,)) < fast_share
    fast_rate = 1.0 / jax.random.uniform(random_subkeys[1], (HEAD_TOTAL,), minval=30.0, maxval=50.0)
    slow_rate = jax.random.uniform(random_subkeys[2], (HEAD_TOTAL,), minval=0.2, maxval=0.6) / DOCUMENT_LENGTH
    base_rate = jnp.where(is_fast, fast_rate, slow_rate)
    blocks = DOCUMENT_LENGTH // TOK_DEV
    device_factor = jnp.exp(jax.random.uniform(random_subkeys[3], (blocks, 1, HEAD_TOTAL), minval=-0.4, maxval=0.4))
    token_factor = jnp.exp(jax.random.uniform(random_subkeys[4], (blocks, TOK_DEV, HEAD_TOTAL), minval=-0.7, maxval=0.7))
    decay_speed = (base_rate * device_factor * token_factor).reshape(DOCUMENT_LENGTH, HEAD_TOTAL)
    spike_position = jax.random.randint(random_subkeys[5], (2, HEAD_TOTAL), 0, DOCUMENT_LENGTH)
    spike_magnitude = jnp.log(jax.random.uniform(random_subkeys[6], (2, HEAD_TOTAL), minval=0.5, maxval=0.8))
    token_locations = jnp.arange(DOCUMENT_LENGTH)[:, None]
    spike_events = jnp.where(token_locations == spike_position[0], spike_magnitude[0], 0.0) + jnp.where(token_locations == spike_position[1], spike_magnitude[1], 0.0)
    return (spike_events - decay_speed).astype(jnp.float32)


def levels(rng, shape, cuts, least, top_value):
    def one(dim, parts):
        draws = jax.random.uniform(jax.random.fold_in(jax.random.fold_in(rng, 6), dim), (parts,), jnp.float32, least / len(cuts), top_value / len(cuts))
        return jnp.repeat(jnp.exp(draws), shape[dim] // parts).reshape((-1,) + (1,) * (len(shape) - dim - 1))

    level = one(*cuts[0])
    for cut in cuts[1:]:
        level = level * one(*cut)
    return level


def centred(rng, extent, scale, limit, pieces=(), kind=jnp.bfloat16):
    entries = jax.random.normal(rng, extent, jnp.float32) * scale
    if len(pieces) > 0:
        entries = levels(rng, extent, pieces, -0.22, 0.18) * entries
    return jnp.clip(entries, min=-limit, max=limit).astype(kind)


def setup_inputs(seed: int = 0) -> dict:
    seeds = jax.random.split(jax.random.key(seed), 13)
    return {
        "hidden": centred(seeds[0], (DOCUMENT_LENGTH, D), 1.0, 6.0, ((0, 8), (1, 4))),
        "norm_gain": jnp.clip(1.0 + 0.18 * jax.random.normal(seeds[1], (D,), jnp.float32), 0.1, 1.9),
        "zx_weight": centred(seeds[2], (D, 2, INNER), D ** -0.5, 0.15625, ((2, 4),)),
        "bc_weight": centred(seeds[3], (D, 2 * STATE), D ** -0.5, 0.15625),
        "dt_weight": centred(seeds[4], (D, HEAD_TOTAL), D ** -0.5, 0.15625, ((1, 4),)),
        "conv_x": jnp.clip(jax.random.uniform(seeds[5], (CONV + 1, INNER), jnp.float32, -0.5, 0.5) * levels(seeds[5], (CONV + 1, INNER), ((1, 4),), -0.4, 0.0), -0.5, 0.5),
        "conv_bc": jnp.clip(jax.random.uniform(seeds[6], (CONV + 1, 2 * STATE), jnp.float32, -0.5, 0.5), -0.5, 0.5),
        "dt_bias": jnp.clip(-4.6 + 2.3 * jax.random.uniform(seeds[7], (HEAD_TOTAL,), jnp.float32) ** levels(seeds[7], (HEAD_TOTAL,), ((0, 4),), -0.2, 0.2), -4.6, -2.3),
        "log_decay": draw_log_decay(jax.random.fold_in(seeds[12], 71), 0),
        "skip_gain": jnp.clip(jnp.exp(math.log(2.0) - 1.3862944 * jax.random.uniform(seeds[9], (HEAD_TOTAL,), jnp.float32) ** levels(seeds[9], (HEAD_TOTAL,), ((0, 4),), -0.2, 0.2)), 0.5, 2.0),
        "out_gain": jnp.clip(1.0 + 0.18 * jax.random.normal(seeds[10], (INNER,), jnp.float32), 0.1, 1.9),
        "out_weight": centred(seeds[11], (INNER, D), INNER ** -0.5, 0.109375, ((0, 4),)),
    }


eps = 1e-05

def convolve(extended, conv_taps):
    tap_count = conv_taps.shape[0] - 1
    out_rows = extended.shape[0] - tap_count + 1
    summed_taps = conv_taps[tap_count]
    for offset in range(tap_count):
        summed_taps = summed_taps + conv_taps[offset] * extended[offset:offset + out_rows].astype(jnp.float32)
    return jax.nn.silu(summed_taps).astype(jnp.bfloat16)

def reference(hidden, norm_gain, zx_weight, bc_weight, dt_weight, conv_x, conv_bc, dt_bias, log_decay, skip_gain, out_gain, out_weight):
    rim_rows = CONV - 1
    position = jnp.arange(BLOCK)
    causal = position[:, None] >= position[None, :]
    group_width = INNER // N_HEAD
    highest = lax.Precision.HIGHEST

    def advance(carry_in, block_in):
        previous_raw, state = carry_in
        row_block, decay_rows = block_in
        values = row_block.astype(jnp.float32)
        mean_square = lax.optimization_barrier(jnp.mean(values * values, axis=-1, keepdims=True))
        normed = (values * lax.rsqrt(mean_square + eps) * norm_gain).astype(jnp.bfloat16)
        gate_raw = jnp.dot(normed, zx_weight[:, 0, :], preferred_element_type=jnp.float32).astype(jnp.bfloat16)
        x_raw = jnp.dot(normed, zx_weight[:, 1, :], preferred_element_type=jnp.float32).astype(jnp.bfloat16)
        bc_raw = jnp.dot(normed, bc_weight, preferred_element_type=jnp.float32).astype(jnp.bfloat16)
        step_raw = jnp.dot(normed, dt_weight, preferred_element_type=jnp.float32).astype(jnp.bfloat16)
        projected = jnp.concatenate([x_raw, bc_raw], axis=1)
        extended = jnp.concatenate([previous_raw, projected], axis=0)
        x_conv = convolve(extended[:, :INNER], conv_x)
        bc_conv = convolve(extended[:, INNER:], conv_bc)
        b_rows = bc_conv[:, :STATE]
        c_rows = bc_conv[:, STATE:]
        step_size = jax.nn.softplus(step_raw.astype(jnp.float32) + dt_bias)
        decay_sum = jnp.cumsum(decay_rows, axis=0)
        decay_t = decay_sum.T
        step_t = step_size.T
        scores = jnp.dot(c_rows, b_rows.T, preferred_element_type=jnp.float32)
        log_gap = jnp.where(causal, decay_t[:, :, None] - decay_t[:, None, :], 0.0)
        mix_weights = jnp.where(causal, scores[None] * jnp.exp(log_gap) * step_t[:, None, :], 0.0).astype(jnp.bfloat16)
        x_heads = x_conv.reshape(BLOCK, HEAD_TOTAL, HEADDIM).astype(jnp.float32)
        y_inside = jnp.einsum('hts,shp->thp', mix_weights.astype(jnp.float32), x_heads, precision=highest)
        c_wide = c_rows.astype(jnp.float32)
        b_wide = b_rows.astype(jnp.float32)
        y_carried = jnp.exp(decay_sum)[:, :, None] * jnp.einsum('tn,hpn->thp', c_wide, state, precision=highest)
        to_end = jnp.exp(decay_t[:, -1:] - decay_t) * step_t
        weighted = x_heads * to_end.T[:, :, None]
        block_state = jnp.einsum('shp,sn->hpn', weighted, b_wide, precision=highest)
        new_state = jnp.exp(decay_t[:, -1])[:, None, None] * state + block_state
        y_heads = y_inside + y_carried + skip_gain[None, :, None] * x_heads
        gated = y_heads.reshape(BLOCK, INNER) * jax.nn.silu(gate_raw.astype(jnp.float32))
        square_mean = lax.optimization_barrier(jnp.mean(gated * gated, axis=-1, keepdims=True))
        y_normed = (gated * lax.rsqrt(square_mean + eps) * out_gain).astype(jnp.bfloat16)
        summed = jnp.zeros((BLOCK, D), jnp.float32)
        for group in range(N_HEAD):
            piece = jnp.dot(y_normed[:, group * group_width:(group + 1) * group_width], out_weight[group * group_width:(group + 1) * group_width], preferred_element_type=jnp.float32).astype(jnp.bfloat16)
            piece = lax.optimization_barrier(piece)
            summed = summed + piece.astype(jnp.float32)
        return ((extended[extended.shape[0] - rim_rows:], new_state), summed.astype(jnp.bfloat16))
    start_carry = (jnp.zeros((rim_rows, INNER + 2 * STATE), jnp.bfloat16), jnp.zeros((HEAD_TOTAL, HEADDIM, STATE), jnp.float32))
    block_total = DOCUMENT_LENGTH // BLOCK
    unused, outputs = lax.scan(advance, start_carry, (hidden.reshape(block_total, BLOCK, D), log_decay.reshape(block_total, BLOCK, HEAD_TOTAL)))
    return outputs.reshape(DOCUMENT_LENGTH, D)
```

```python
import functools

import jax
import jax.numpy as jnp
from jax import lax
from jax.experimental import pallas as pl
from jax.experimental.pallas import tpu as pltpu
from jax.sharding import PartitionSpec as P

HEADDIM = 64
STATE = 128
CONV = 4
BLOCK = 256
HALO = 16
QUAD = 256
PER = QUAD // HEADDIM

eps = 1e-05
F32 = jnp.float32
BF16 = jnp.bfloat16


def dot(a, b):
    return jnp.dot(a, b, preferred_element_type=F32)


def silu(v):
    return v / (1.0 + jnp.exp(-v))


def spread(column_of, first, lane, rows):
    out = None
    for k in range(PER):
        piece = jnp.broadcast_to(column_of(first + k), (rows, QUAD))
        out = piece if out is None else jnp.where(lane >= k * HEADDIM, piece, out)
    return out


def kernel(
    places,
    hidden,
    wzx_hbm,
    wbc_hbm,
    wout_hbm,
    gain,
    wdt_in,
    taps_x,
    taps_bc,
    dtb,
    ld_in,
    skip,
    out_gain,
    out,
    xg,
    wzx,
    wbc,
    wout,
    wdt,
    nrm,
    tail,
    ldp,
    gate,
    xc,
    cm,
    yi,
    ent,
    tl,
    ed,
    st,
    dsum,
    got_s,
    got_d,
    snd_s,
    snd_d,
    got_e,
    snd_e,
    back,
    inc,
    gb,
    send_p,
    recv_p,
    own,
    send_y,
    recv_y,
    sq,
    load_sem,
    ys,
    yr,
    ps,
    pr,
    fs,
    fr,
    hs,
    hr,
    cs,
    cr,
    es,
    er,
    bs,
    br,
    rs,
    rr,
    zs,
    zr,
    qs,
    qr,
):
    places_ctx = places
    rows, feat = hidden.shape
    width = 4 * feat
    inner = wzx.shape[1] // 2
    heads = inner // HEADDIM
    quads = inner // QUAD
    chunks = rows // BLOCK
    ctx = lax.axis_index("ctx")
    me = lax.axis_index("head")
    partner = me + 1 - 2 * lax.rem(me, 2)
    other = lax.rem(me + 2, 4)
    diag = lax.rem(partner + 2, 4)
    odd = lax.rem(ctx, 2)
    MESH = pl.DeviceIdType.MESH

    def remote(src, dst, ss, rsem, c, h):
        return pltpu.make_async_remote_copy(
            src_ref=src, dst_ref=dst, send_sem=ss, recv_sem=rsem, device_id=(c, h), device_id_type=MESH
        )

    own_load = pltpu.make_async_copy(hidden, xg.at[me, pl.ds(HALO, rows)], load_sem.at[0])
    loads = [
        pltpu.make_async_copy(wbc_hbm, wbc, load_sem.at[1]),
        pltpu.make_async_copy(wzx_hbm, wzx, load_sem.at[2]),
    ]
    out_load = pltpu.make_async_copy(wout_hbm, wout, load_sem.at[3])

    barrier = pltpu.get_barrier_semaphore()

    def greet(c, h):
        pl.semaphore_signal(barrier, inc=1, device_id=(c, h), device_id_type=MESH)

    for h in (partner, other, diag):
        greet(ctx, h)

    @pl.when(ctx > 0)
    def _():
        for h in range(4):
            greet(ctx - 1, h)

    @pl.when(ctx < places_ctx - 1)
    def _():
        for h in range(4):
            greet(ctx + 1, h)

    @pl.when(ctx >= 2)
    def _():
        greet(ctx - 2, me)

    @pl.when(ctx < places_ctx - 2)
    def _():
        greet(ctx + 2, me)

    own_load.start()
    for load in loads:
        load.start()
    out_load.start()
    below = lax.div(ctx + places_ctx - 1, places_ctx)
    above = lax.div(2 * places_ctx - 2 - ctx, places_ctx)
    two_below = lax.div(ctx + places_ctx - 2, places_ctx)
    two_above = lax.div(2 * places_ctx - 3 - ctx, places_ctx)
    pl.semaphore_wait(barrier, 3 + 4 * (below + above) + two_below + two_above)

    def src_rows(c):
        return hidden.at[pl.ds(pl.multiple_of(c * BLOCK, BLOCK), BLOCK)]

    def slot(h, c):
        return xg.at[h, pl.ds(pl.multiple_of(HALO + c * BLOCK, HALO), BLOCK)]

    def to_y(c):
        return remote(src_rows(c), slot(me, c), ys.at[c], yr.at[c], ctx, other)

    def to_p(c):
        return remote(src_rows(c), slot(me, c), ps.at[c], pr.at[c], ctx, partner)

    def forward(c):
        return remote(slot(other, c), slot(other, c), fs.at[c], fr.at[c], ctx, partner)

    def halo(h, sender):
        return remote(
            hidden.at[pl.ds(rows - HALO, HALO)],
            xg.at[sender, pl.ds(0, HALO)],
            hs.at[h],
            hr.at[sender],
            ctx + 1,
            h,
        )

    @pl.when(ctx < places_ctx - 1)
    def _():
        for h in range(4):
            halo(h, me).start()

    for c in range(chunks):
        to_y(c).start()
    for c in range(chunks):
        to_p(c).start()

    @pl.when(ctx == 0)
    def _():
        xg[:, 0:HALO, :] = jnp.zeros((4, HALO, feat), BF16)

    wdt[...] = jnp.zeros_like(wdt)
    wdt[:, 0:heads] = wdt_in[...]
    ldp[...] = jnp.zeros_like(ldp)
    st[...] = jnp.zeros_like(st)
    dsum[...] = jnp.zeros_like(dsum)

    @pl.when(ctx > 0)
    def _():
        for h in range(4):
            halo(0, h).wait_recv()

    for load in loads:
        load.wait()
    own_load.wait()

    def normalised(at, count):
        vals = [xg[j, at, :].astype(F32) for j in range(4)]
        total = sum(jnp.sum(v * v, axis=-1, keepdims=True) for v in vals)
        scale = lax.rsqrt(total / width + eps)
        for j in range(4):
            span = slice(j * feat, (j + 1) * feat)
            nrm[0:count, span] = (vals[j] * scale * gain[:, span]).astype(BF16)

    normalised(pl.ds(0, HALO), HALO)
    head_rows = nrm[0:HALO, :]
    for s in range(quads):
        tail[:, s * QUAD : (s + 1) * QUAD] = dot(
            head_rows, wzx[:, inner + s * QUAD : inner + (s + 1) * QUAD]
        )
    tail[:, inner : inner + 2 * STATE] = dot(head_rows, wbc[...])

    lane = lax.broadcasted_iota(jnp.int32, (1, QUAD), 1)
    row_id = lax.broadcasted_iota(jnp.int32, (BLOCK, BLOCK), 0)
    col_id = lax.broadcasted_iota(jnp.int32, (BLOCK, BLOCK), 1)

    def convolved(raw, span, taps):
        ext = jnp.concatenate([tail[:, span], raw], axis=0)
        summed = taps[CONV : CONV + 1, :] + taps[CONV - 1 : CONV, :] * ext
        for back_by in range(1, CONV):
            at = CONV - 1 - back_by
            summed = summed + taps[at : at + 1, :] * pltpu.roll(ext, back_by, 0)
        tail[:, span] = raw[BLOCK - HALO :, :]
        return silu(summed[HALO:, :])

    def first(c, carry):
        to_y(c).wait_recv()
        forward(c).start()
        to_p(c).wait_recv()
        remote(slot(diag, c), slot(diag, c), fs.at[c], fr.at[c], ctx, partner).wait_recv()
        here = pl.ds(pl.multiple_of(c * BLOCK, BLOCK), BLOCK)
        normalised(pl.ds(pl.multiple_of(HALO + c * BLOCK, HALO), BLOCK), BLOCK)
        normed = nrm[...]
        bc = convolved(dot(normed, wbc[...]), slice(inner, inner + 2 * STATE), taps_bc[...])
        b = bc[:, :STATE].astype(BF16)
        cc = bc[:, STATE:].astype(BF16)
        cm[here, :] = cc
        raw_step = dot(normed, wdt[...]) + dtb[...]
        step = jnp.maximum(raw_step, 0.0) + jnp.log1p(jnp.exp(-jnp.abs(raw_step)))
        ldp[:, 0:heads] = ld_in[here, :]
        tri = jnp.where(row_id >= col_id, 1.0, 0.0).astype(F32)
        dcol = jnp.dot(tri, ldp[...], preferred_element_type=F32, precision=lax.Precision.HIGHEST)
        ed[here, :] = jnp.exp(dcol)
        drow = dcol.T
        srow = step.T
        wrow = jnp.exp(drow[:, BLOCK - 1 : BLOCK] - drow) * srow
        scores = lax.dot_general(
            cc, b, (((1,), (1,)), ((), ())), preferred_element_type=F32
        )
        scores = jnp.where(row_id >= col_id, scores, 0.0)
        b_t = b.astype(F32).T
        for q in range(quads):
            span = slice(q * QUAD, (q + 1) * QUAD)
            gate[here, span] = dot(normed, wzx[:, span]).astype(BF16)
            raw = dot(normed, wzx[:, inner + q * QUAD : inner + (q + 1) * QUAD])
            xq = convolved(raw, span, taps_x[:, span]).astype(BF16)
            xc[here, span] = xq
            y_acc = None
            s_acc = None
            for k in range(PER):
                h = q * PER + k
                gap = jnp.minimum(dcol[:, h : h + 1] - drow[h : h + 1, :], 0.0)
                mix = (scores * jnp.exp(gap) * srow[h : h + 1, :]).astype(BF16)
                wb = (b_t * wrow[h : h + 1, :]).astype(BF16)
                y_h = dot(mix, xq)
                s_h = dot(wb, xq)
                if k == 0:
                    y_acc, s_acc = y_h, s_h
                else:
                    y_acc = jnp.where(lane >= k * HEADDIM, y_h, y_acc)
                    s_acc = jnp.where(lane >= k * HEADDIM, s_h, s_acc)
            yi[here, span] = y_acc
            total = spread(lambda i: dcol[BLOCK - 1 : BLOCK, i : i + 1], q * PER, lane, 1)
            ent[c, :, span] = st[:, span].astype(BF16)
            tl[c, :, span] = dsum[:, span]
            st[:, span] = jnp.exp(total) * st[:, span] + s_acc
            dsum[:, span] = dsum[:, span] + total
        return carry

    lax.fori_loop(0, chunks, first, 0)

    def lanes(q):
        return pl.ds(q * QUAD, QUAD)

    def state_copy(q):
        return remote(snd_s.at[q], got_s.at[q], cs.at[q], cr.at[q], ctx + 1, me)

    decay_copy = remote(snd_d, got_d, cs.at[quads], cr.at[quads], ctx + 1, me)

    def enter_copy(q):
        return remote(snd_e.at[q], got_e.at[q], es.at[q], er.at[q], ctx + 2, me)

    def back_copy(q):
        return remote(got_e.at[q], back.at[q], bs.at[q], br.at[q], ctx - 1, me)

    @pl.when(odd == 0)
    def _():
        snd_d[...] = dsum[...]
        decay_copy.start()
        for q in range(quads):
            snd_s[q] = st[:, q * QUAD : (q + 1) * QUAD].astype(BF16)
            state_copy(q).start()

    @pl.when(odd == 1)
    def _():
        decay_copy.wait_recv()

        @pl.when(ctx < 2)
        def _():
            got_e[...] = jnp.zeros_like(got_e)

        for q in range(quads):
            span = slice(q * QUAD, (q + 1) * QUAD)
            state_copy(q).wait_recv()
            mine = jnp.exp(dsum[0:1, span])
            both = jnp.exp(dsum[0:1, span] + got_d[0:1, span])
            pair = mine * got_s[q].astype(F32) + st[:, span]

            @pl.when(ctx >= 2)
            def _():
                enter_copy(q).wait_recv()
                back_copy(q).start()

            entered = got_e[q].astype(F32)

            @pl.when(ctx < places_ctx - 2)
            def _():
                snd_e[q] = (both * entered + pair).astype(BF16)
                enter_copy(q).start()

            inc[:, span] = jnp.exp(got_d[0:1, span]) * entered + got_s[q].astype(F32)

    @pl.when(odd == 0)
    def _():
        @pl.when(ctx < 2)
        def _():
            inc[...] = jnp.zeros_like(inc)

        @pl.when(ctx >= 2)
        def _():
            for q in range(quads):
                back_copy(q).wait_recv()
                inc[:, q * QUAD : (q + 1) * QUAD] = back[q].astype(F32)

    out_load.wait()

    def piece_copy(c):
        return remote(send_p.at[c], recv_p.at[c], rs.at[c], rr.at[c], ctx, partner)

    def far_copy(c):
        return remote(send_y.at[c], recv_y.at[c], zs.at[c], zr.at[c], ctx, other)

    def square_copy(c, h, k, sender):
        return remote(sq.at[sender, c], sq.at[sender, c], qs.at[k, c], qr.at[k, c], ctx, h)

    def columns(h):
        return pl.ds(pl.multiple_of(h * feat, 128), feat)

    def combine(c):
        piece_copy(c).wait_recv()
        own[c, 0] = own[c, 0] + recv_p[c, 0].astype(F32)
        send_y[c] = (own[c, 1] + recv_p[c, 1].astype(F32)).astype(BF16)
        far_copy(c).start()

    def second(c, carry):
        here = pl.ds(pl.multiple_of(c * BLOCK, BLOCK), BLOCK)
        squares = jnp.zeros((BLOCK, 1), F32)
        e_all = ed[here, :]
        cc = cm[here, :]
        for q in range(quads):
            span = slice(q * QUAD, (q + 1) * QUAD)
            carried = ent[c, :, span].astype(F32) + jnp.exp(tl[c, 0:1, span]) * inc[:, span]
            yc = dot(cc, carried.astype(BF16))
            growth = spread(lambda i: e_all[:, i : i + 1], q * PER, lane, BLOCK)
            y = yi[here, span] + growth * yc + skip[:, span] * xc[here, span].astype(F32)
            gated = y * silu(gate[here, span].astype(F32))
            squares = squares + jnp.sum(gated * gated, axis=-1, keepdims=True)
            gb[:, span] = (gated * out_gain[:, span]).astype(BF16)
        g = gb[...]
        send_p[c, 0] = dot(g, wout[:, columns(partner)]).astype(BF16)
        send_p[c, 1] = dot(g, wout[:, columns(diag)]).astype(BF16)
        piece_copy(c).start()
        sq[me, c] = jnp.broadcast_to(squares, (BLOCK, 128)).T[0:8, :]
        for k, h in enumerate((partner, other, diag)):
            square_copy(c, h, k, me).start()
        own[c, 1] = dot(g, wout[:, columns(other)])
        own[c, 0] = dot(g, wout[:, columns(me)])

        @pl.when(c > 0)
        def _():
            combine(c - 1)

        return carry

    lax.fori_loop(0, chunks, second, 0)
    combine(chunks - 1)

    def third(c, carry):
        here = pl.ds(pl.multiple_of(c * BLOCK, BLOCK), BLOCK)
        for k, h in enumerate((partner, other, diag)):
            square_copy(c, h, k, h).wait_recv()
        total = (sq[0, c] + sq[1, c]) + (sq[2, c] + sq[3, c])
        scale_row = lax.rsqrt(total / (4 * inner) + eps)
        scale = jnp.broadcast_to(scale_row[0:1, :], (128, BLOCK)).T[:, 0:1]
        far_copy(c).wait_recv()
        out[here, :] = ((own[c, 0] + recv_y[c].astype(F32)) * scale).astype(BF16)
        return carry

    lax.fori_loop(0, chunks, third, 0)

    for c in range(chunks):
        to_y(c).wait_send()
        to_p(c).wait_send()
        forward(c).wait_send()
        piece_copy(c).wait_send()
        far_copy(c).wait_send()
        for k, h in enumerate((partner, other, diag)):
            square_copy(c, h, k, me).wait_send()

    @pl.when(ctx < places_ctx - 1)
    def _():
        for h in range(4):
            halo(h, me).wait_send()

    @pl.when(odd == 0)
    def _():
        decay_copy.wait_send()
        for q in range(quads):
            state_copy(q).wait_send()

    @pl.when(odd == 1)
    def _():
        @pl.when(ctx >= 2)
        def _():
            for q in range(quads):
                back_copy(q).wait_send()

        @pl.when(ctx < places_ctx - 2)
        def _():
            for q in range(quads):
                enter_copy(q).wait_send()


def per_device(
    places,
    hidden,
    norm_gain,
    zx_weight,
    bc_weight,
    dt_weight,
    conv_x,
    conv_bc,
    dt_bias,
    log_decay,
    skip_gain,
    out_gain,
    out_weight,
):
    rows, feat = hidden.shape
    width = zx_weight.shape[0]
    inner = zx_weight.shape[2]
    heads = dt_weight.shape[1]
    quads = inner // QUAD
    chunks = rows // BLOCK
    any_spec = pl.BlockSpec(memory_space=pl.ANY)
    vmem = pl.BlockSpec(memory_space=pltpu.VMEM)
    dma = pltpu.SemaphoreType.DMA
    return pl.pallas_call(
        functools.partial(kernel, places),
        out_shape=jax.ShapeDtypeStruct((rows, feat), BF16),
        in_specs=[any_spec] * 4 + [vmem] * 8,
        out_specs=vmem,
        scratch_shapes=[
            pltpu.VMEM((4, HALO + rows, feat), BF16),
            pltpu.VMEM((width, 2 * inner), BF16),
            pltpu.VMEM((width, 2 * STATE), BF16),
            pltpu.VMEM((inner, width), BF16),
            pltpu.VMEM((width, 128), BF16),
            pltpu.VMEM((BLOCK, width), BF16),
            pltpu.VMEM((HALO, inner + 2 * STATE), F32),
            pltpu.VMEM((BLOCK, 128), F32),
            pltpu.VMEM((rows, inner), BF16),
            pltpu.VMEM((rows, inner), BF16),
            pltpu.VMEM((rows, STATE), BF16),
            pltpu.VMEM((rows, inner), F32),
            pltpu.VMEM((chunks, STATE, inner), BF16),
            pltpu.VMEM((chunks, 8, inner), F32),
            pltpu.VMEM((rows, 128), F32),
            pltpu.VMEM((STATE, inner), F32),
            pltpu.VMEM((8, inner), F32),
            pltpu.VMEM((quads, STATE, QUAD), BF16),
            pltpu.VMEM((8, inner), F32),
            pltpu.VMEM((quads, STATE, QUAD), BF16),
            pltpu.VMEM((8, inner), F32),
            pltpu.VMEM((quads, STATE, QUAD), BF16),
            pltpu.VMEM((quads, STATE, QUAD), BF16),
            pltpu.VMEM((quads, STATE, QUAD), BF16),
            pltpu.VMEM((STATE, inner), F32),
            pltpu.VMEM((BLOCK, inner), BF16),
            pltpu.VMEM((chunks, 2, BLOCK, feat), BF16),
            pltpu.VMEM((chunks, 2, BLOCK, feat), BF16),
            pltpu.VMEM((chunks, 2, BLOCK, feat), F32),
            pltpu.VMEM((chunks, BLOCK, feat), BF16),
            pltpu.VMEM((chunks, BLOCK, feat), BF16),
            pltpu.VMEM((4, chunks, 8, BLOCK), F32),
            dma((4,)),
            dma((chunks,)),
            dma((chunks,)),
            dma((chunks,)),
            dma((chunks,)),
            dma((chunks,)),
            dma((chunks,)),
            dma((4,)),
            dma((4,)),
            dma((quads + 1,)),
            dma((quads + 1,)),
            dma((quads,)),
            dma((quads,)),
            dma((quads,)),
            dma((quads,)),
            dma((chunks,)),
            dma((chunks,)),
            dma((chunks,)),
            dma((chunks,)),
            dma((3, chunks)),
            dma((3, chunks)),
        ],
        compiler_params=pltpu.CompilerParams(
            collective_id=0, has_side_effects=True, vmem_limit_bytes=63000000
        ),
        name="mixer",
    )(
        hidden,
        zx_weight.reshape(width, 2 * inner),
        bc_weight,
        out_weight,
        norm_gain.reshape(1, width),
        dt_weight,
        conv_x,
        conv_bc,
        jnp.pad(dt_bias, (0, 128 - heads)).reshape(1, 128),
        log_decay,
        jnp.repeat(skip_gain, HEADDIM).reshape(1, inner),
        out_gain.reshape(1, inner),
    )


def solution(mesh):
    placed = (
        P("ctx", "head"),
        P(),
        P(None, None, "head"),
        P(),
        P(None, "head"),
        P(None, "head"),
        P(),
        P("head"),
        P("ctx", "head"),
        P("head"),
        P("head"),
        P("head", None),
    )
    return jax.shard_map(
        functools.partial(per_device, mesh.shape["ctx"]),
        mesh=mesh,
        in_specs=placed,
        out_specs=P("ctx", "head"),
        check_vma=False,
    )
```

```python
import functools

import jax
import jax.numpy as jnp
from jax import lax
from jax.experimental import pallas as pl
from jax.experimental.pallas import tpu as pltpu
from jax.sharding import PartitionSpec as P

HEADDIM = 64
STATE = 128
CONV = 4
BLOCK = 256
HALO = 16
QUAD = 256
PER = QUAD // HEADDIM

eps = 1e-05
F32 = jnp.float32
BF16 = jnp.bfloat16


def dot(a, b):
    return jnp.dot(a, b, preferred_element_type=F32)


def silu(v):
    return v / (1.0 + jnp.exp(-v))


def spread(column_of, first, lane, rows):
    out = None
    for k in range(PER):
        piece = jnp.broadcast_to(column_of(first + k), (rows, QUAD))
        out = piece if out is None else jnp.where(lane >= k * HEADDIM, piece, out)
    return out


def kernel(
    places,
    hidden,
    wzx_hbm,
    wbc_hbm,
    wout_hbm,
    gain,
    wdt_in,
    taps_x,
    taps_bc,
    dtb,
    ld_in,
    skip,
    out_gain,
    out,
    xg,
    wraw,
    wzx,
    wbc,
    wout,
    wdt,
    dtrow,
    skrow,
    nrm,
    tail,
    ldp,
    gate,
    xc,
    cm,
    yi,
    ent,
    tl,
    ed,
    st,
    dsum,
    got_s,
    got_d,
    snd_s,
    snd_d,
    got_e,
    snd_e,
    back,
    inc,
    gb,
    send_p,
    recv_p,
    own,
    send_y,
    recv_y,
    sq,
    load_sem,
    ys,
    yr,
    ps,
    pr,
    fs,
    fr,
    hs,
    hr,
    cs,
    cr,
    es,
    er,
    bs,
    br,
    rs,
    rr,
    zs,
    zr,
    qs,
    qr,
):
    places_ctx = places
    rows, feat = hidden.shape
    width = 4 * feat
    inner = wzx.shape[1] // 2
    heads = inner // HEADDIM
    quads = inner // QUAD
    chunks = rows // BLOCK
    ctx = lax.axis_index("ctx")
    me = lax.axis_index("head")
    partner = me + 1 - 2 * lax.rem(me, 2)
    other = lax.rem(me + 2, 4)
    diag = lax.rem(partner + 2, 4)
    odd = lax.rem(ctx, 2)
    MESH = pl.DeviceIdType.MESH

    def remote(src, dst, ss, rsem, c, h):
        return pltpu.make_async_remote_copy(
            src_ref=src, dst_ref=dst, send_sem=ss, recv_sem=rsem, device_id=(c, h), device_id_type=MESH
        )

    own_load = pltpu.make_async_copy(hidden, xg.at[me, pl.ds(HALO, rows)], load_sem.at[0])
    loads = [
        pltpu.make_async_copy(wbc_hbm, wbc, load_sem.at[1]),
        pltpu.make_async_copy(wzx_hbm, wraw, load_sem.at[2]),
    ]
    out_load = pltpu.make_async_copy(wout_hbm, wout, load_sem.at[3])

    barrier = pltpu.get_barrier_semaphore()

    def greet(c, h):
        pl.semaphore_signal(barrier, inc=1, device_id=(c, h), device_id_type=MESH)

    for h in (partner, other, diag):
        greet(ctx, h)

    @pl.when(ctx > 0)
    def _():
        for h in range(4):
            greet(ctx - 1, h)

    @pl.when(ctx < places_ctx - 1)
    def _():
        for h in range(4):
            greet(ctx + 1, h)

    @pl.when(ctx >= 2)
    def _():
        greet(ctx - 2, me)

    @pl.when(ctx < places_ctx - 2)
    def _():
        greet(ctx + 2, me)

    own_load.start()
    for load in loads:
        load.start()
    out_load.start()
    below = lax.div(ctx + places_ctx - 1, places_ctx)
    above = lax.div(2 * places_ctx - 2 - ctx, places_ctx)
    two_below = lax.div(ctx + places_ctx - 2, places_ctx)
    two_above = lax.div(2 * places_ctx - 3 - ctx, places_ctx)
    pl.semaphore_wait(barrier, 3 + 4 * (below + above) + two_below + two_above)

    def src_rows(c):
        return hidden.at[pl.ds(pl.multiple_of(c * BLOCK, BLOCK), BLOCK)]

    def slot(h, c):
        return xg.at[h, pl.ds(pl.multiple_of(HALO + c * BLOCK, HALO), BLOCK)]

    def to_y(c):
        return remote(src_rows(c), slot(me, c), ys.at[c], yr.at[c], ctx, other)

    def to_p(c):
        return remote(src_rows(c), slot(me, c), ps.at[c], pr.at[c], ctx, partner)

    def forward(c):
        return remote(slot(other, c), slot(other, c), fs.at[c], fr.at[c], ctx, partner)

    def halo(h, sender):
        return remote(
            hidden.at[pl.ds(rows - HALO, HALO)],
            xg.at[sender, pl.ds(0, HALO)],
            hs.at[h],
            hr.at[sender],
            ctx + 1,
            h,
        )

    @pl.when(ctx < places_ctx - 1)
    def _():
        for h in range(4):
            halo(h, me).start()

    for c in range(chunks):
        to_y(c).start()
    for c in range(chunks):
        to_p(c).start()

    @pl.when(ctx == 0)
    def _():
        xg[:, 0:HALO, :] = jnp.zeros((4, HALO, feat), BF16)

    dt_wide = jnp.concatenate(
        [wdt_in[...].astype(F32), jnp.zeros((128 - heads, width), F32)], axis=0
    )
    wdt[...] = dt_wide.T.astype(BF16)
    few = lax.broadcasted_iota(jnp.int32, (8, 128), 1)
    bias_row = jnp.zeros((8, 128), F32)
    for h in range(heads):
        bias_row = jnp.where(few == h, dtb[h], bias_row)
    dtrow[...] = bias_row
    wide = lax.broadcasted_iota(jnp.int32, (8, inner), 1)
    skip_row = jnp.zeros((8, inner), F32)
    for h in range(heads):
        skip_row = jnp.where(wide >= h * HEADDIM, skip[h], skip_row)
    skrow[...] = skip_row
    ldp[...] = jnp.zeros_like(ldp)
    st[...] = jnp.zeros_like(st)
    dsum[...] = jnp.zeros_like(dsum)

    @pl.when(ctx > 0)
    def _():
        for h in range(4):
            halo(0, h).wait_recv()

    for load in loads:
        load.wait()
    own_load.wait()

    def split(i, carry):
        at = pl.ds(pl.multiple_of(i * 64, 64), 64)
        both = wraw[at, :, :]
        wzx[at, 0:inner] = both[:, 0, :]
        wzx[at, inner : 2 * inner] = both[:, 1, :]
        return carry

    lax.fori_loop(0, width // 64, split, 0)

    def normalised(at, count):
        vals = [xg[j, at, :].astype(F32) for j in range(4)]
        total = sum(jnp.sum(v * v, axis=-1, keepdims=True) for v in vals)
        scale = lax.rsqrt(total / width + eps)
        for j in range(4):
            span = slice(j * feat, (j + 1) * feat)
            nrm[0:count, span] = (vals[j] * scale * gain[span].reshape(1, feat)).astype(BF16)

    normalised(pl.ds(0, HALO), HALO)
    head_rows = nrm[0:HALO, :]
    for s in range(quads):
        tail[:, s * QUAD : (s + 1) * QUAD] = dot(
            head_rows, wzx[:, inner + s * QUAD : inner + (s + 1) * QUAD]
        )
    tail[:, inner : inner + 2 * STATE] = dot(head_rows, wbc[...])

    lane = lax.broadcasted_iota(jnp.int32, (1, QUAD), 1)
    row_id = lax.broadcasted_iota(jnp.int32, (BLOCK, BLOCK), 0)
    col_id = lax.broadcasted_iota(jnp.int32, (BLOCK, BLOCK), 1)

    def convolved(raw, span, taps):
        ext = jnp.concatenate([tail[:, span], raw], axis=0)
        summed = taps[CONV : CONV + 1, :] + taps[CONV - 1 : CONV, :] * ext
        for back_by in range(1, CONV):
            at = CONV - 1 - back_by
            summed = summed + taps[at : at + 1, :] * pltpu.roll(ext, back_by, 0)
        tail[:, span] = raw[BLOCK - HALO :, :]
        return silu(summed[HALO:, :])

    def first(c, carry):
        to_y(c).wait_recv()
        forward(c).start()
        to_p(c).wait_recv()
        remote(slot(diag, c), slot(diag, c), fs.at[c], fr.at[c], ctx, partner).wait_recv()
        here = pl.ds(pl.multiple_of(c * BLOCK, BLOCK), BLOCK)
        normalised(pl.ds(pl.multiple_of(HALO + c * BLOCK, HALO), BLOCK), BLOCK)
        normed = nrm[...]
        bc = convolved(dot(normed, wbc[...]), slice(inner, inner + 2 * STATE), taps_bc[...])
        b = bc[:, :STATE].astype(BF16)
        cc = bc[:, STATE:].astype(BF16)
        cm[here, :] = cc
        raw_step = dot(normed, wdt[...]) + dtrow[0:1, :]
        step = jnp.maximum(raw_step, 0.0) + jnp.log1p(jnp.exp(-jnp.abs(raw_step)))
        ldp[0:heads, :] = ld_in[:, here]
        tri = jnp.where(row_id <= col_id, 1.0, 0.0).astype(F32)
        drow = jnp.dot(ldp[...], tri, preferred_element_type=F32, precision=lax.Precision.HIGHEST)
        dcol = drow.T
        ed[here, :] = jnp.exp(dcol)
        srow = step.T
        wrow = jnp.exp(drow[:, BLOCK - 1 : BLOCK] - drow) * srow
        scores = lax.dot_general(
            cc, b, (((1,), (1,)), ((), ())), preferred_element_type=F32
        )
        scores = jnp.where(row_id >= col_id, scores, 0.0)
        b_t = b.astype(F32).T
        for q in range(quads):
            span = slice(q * QUAD, (q + 1) * QUAD)
            gate[here, span] = dot(normed, wzx[:, span]).astype(BF16)
            raw = dot(normed, wzx[:, inner + q * QUAD : inner + (q + 1) * QUAD])
            xq = convolved(raw, span, taps_x[:, span]).astype(BF16)
            xc[here, span] = xq
            y_acc = None
            s_acc = None
            for k in range(PER):
                h = q * PER + k
                gap = jnp.minimum(dcol[:, h : h + 1] - drow[h : h + 1, :], 0.0)
                mix = (scores * jnp.exp(gap) * srow[h : h + 1, :]).astype(BF16)
                wb = (b_t * wrow[h : h + 1, :]).astype(BF16)
                y_h = dot(mix, xq)
                s_h = dot(wb, xq)
                if k == 0:
                    y_acc, s_acc = y_h, s_h
                else:
                    y_acc = jnp.where(lane >= k * HEADDIM, y_h, y_acc)
                    s_acc = jnp.where(lane >= k * HEADDIM, s_h, s_acc)
            yi[here, span] = y_acc
            total = spread(lambda i: dcol[BLOCK - 1 : BLOCK, i : i + 1], q * PER, lane, 1)
            ent[c, :, span] = st[:, span].astype(BF16)
            tl[c, :, span] = dsum[:, span]
            st[:, span] = jnp.exp(total) * st[:, span] + s_acc
            dsum[:, span] = dsum[:, span] + total
        return carry

    lax.fori_loop(0, chunks, first, 0)

    def lanes(q):
        return pl.ds(q * QUAD, QUAD)

    def state_copy(q):
        return remote(snd_s.at[q], got_s.at[q], cs.at[q], cr.at[q], ctx + 1, me)

    decay_copy = remote(snd_d, got_d, cs.at[quads], cr.at[quads], ctx + 1, me)

    def enter_copy(q):
        return remote(snd_e.at[q], got_e.at[q], es.at[q], er.at[q], ctx + 2, me)

    def back_copy(q):
        return remote(got_e.at[q], back.at[q], bs.at[q], br.at[q], ctx - 1, me)

    @pl.when(odd == 0)
    def _():
        snd_d[...] = dsum[...]
        decay_copy.start()
        for q in range(quads):
            snd_s[q] = st[:, q * QUAD : (q + 1) * QUAD].astype(BF16)
            state_copy(q).start()

    @pl.when(odd == 1)
    def _():
        decay_copy.wait_recv()

        @pl.when(ctx < 2)
        def _():
            got_e[...] = jnp.zeros_like(got_e)

        for q in range(quads):
            span = slice(q * QUAD, (q + 1) * QUAD)
            state_copy(q).wait_recv()
            mine = jnp.exp(dsum[0:1, span])
            both = jnp.exp(dsum[0:1, span] + got_d[0:1, span])
            pair = mine * got_s[q].astype(F32) + st[:, span]

            @pl.when(ctx >= 2)
            def _():
                enter_copy(q).wait_recv()
                back_copy(q).start()

            entered = got_e[q].astype(F32)

            @pl.when(ctx < places_ctx - 2)
            def _():
                snd_e[q] = (both * entered + pair).astype(BF16)
                enter_copy(q).start()

            inc[:, span] = jnp.exp(got_d[0:1, span]) * entered + got_s[q].astype(F32)

    @pl.when(odd == 0)
    def _():
        @pl.when(ctx < 2)
        def _():
            inc[...] = jnp.zeros_like(inc)

        @pl.when(ctx >= 2)
        def _():
            for q in range(quads):
                back_copy(q).wait_recv()
                inc[:, q * QUAD : (q + 1) * QUAD] = back[q].astype(F32)

    out_load.wait()

    def piece_copy(c):
        return remote(send_p.at[c], recv_p.at[c], rs.at[c], rr.at[c], ctx, partner)

    def far_copy(c):
        return remote(send_y.at[c], recv_y.at[c], zs.at[c], zr.at[c], ctx, other)

    def square_copy(c, h, k, sender):
        return remote(sq.at[sender, c], sq.at[sender, c], qs.at[k, c], qr.at[k, c], ctx, h)

    def columns(h):
        return pl.ds(pl.multiple_of(h * feat, 128), feat)

    def combine(c):
        piece_copy(c).wait_recv()
        own[c, 0] = own[c, 0] + recv_p[c, 0].astype(F32)
        send_y[c] = (own[c, 1] + recv_p[c, 1].astype(F32)).astype(BF16)
        far_copy(c).start()

    def second(c, carry):
        here = pl.ds(pl.multiple_of(c * BLOCK, BLOCK), BLOCK)
        squares = jnp.zeros((BLOCK, 1), F32)
        e_all = ed[here, :]
        cc = cm[here, :]
        for q in range(quads):
            span = slice(q * QUAD, (q + 1) * QUAD)
            carried = ent[c, :, span].astype(F32) + jnp.exp(tl[c, 0:1, span]) * inc[:, span]
            yc = dot(cc, carried.astype(BF16))
            growth = spread(lambda i: e_all[:, i : i + 1], q * PER, lane, BLOCK)
            y = yi[here, span] + growth * yc + skrow[0:1, span] * xc[here, span].astype(F32)
            gated = y * silu(gate[here, span].astype(F32))
            squares = squares + jnp.sum(gated * gated, axis=-1, keepdims=True)
            gb[:, span] = (gated * out_gain[span].reshape(1, QUAD)).astype(BF16)
        g = gb[...]
        send_p[c, 0] = dot(g, wout[:, columns(partner)]).astype(BF16)
        send_p[c, 1] = dot(g, wout[:, columns(diag)]).astype(BF16)
        piece_copy(c).start()
        sq[me, c] = jnp.broadcast_to(squares, (BLOCK, 128)).T[0:8, :]
        for k, h in enumerate((partner, other, diag)):
            square_copy(c, h, k, me).start()
        own[c, 1] = dot(g, wout[:, columns(other)])
        own[c, 0] = dot(g, wout[:, columns(me)])

        @pl.when(c > 0)
        def _():
            combine(c - 1)

        return carry

    lax.fori_loop(0, chunks, second, 0)
    combine(chunks - 1)

    def third(c, carry):
        here = pl.ds(pl.multiple_of(c * BLOCK, BLOCK), BLOCK)
        for k, h in enumerate((partner, other, diag)):
            square_copy(c, h, k, h).wait_recv()
        total = (sq[0, c] + sq[1, c]) + (sq[2, c] + sq[3, c])
        scale_row = lax.rsqrt(total / (4 * inner) + eps)
        scale = jnp.broadcast_to(scale_row[0:1, :], (128, BLOCK)).T[:, 0:1]
        far_copy(c).wait_recv()
        out[here, :] = ((own[c, 0] + recv_y[c].astype(F32)) * scale).astype(BF16)
        return carry

    lax.fori_loop(0, chunks, third, 0)

    for c in range(chunks):
        to_y(c).wait_send()
        to_p(c).wait_send()
        forward(c).wait_send()
        piece_copy(c).wait_send()
        far_copy(c).wait_send()
        for k, h in enumerate((partner, other, diag)):
            square_copy(c, h, k, me).wait_send()

    @pl.when(ctx < places_ctx - 1)
    def _():
        for h in range(4):
            halo(h, me).wait_send()

    @pl.when(odd == 0)
    def _():
        decay_copy.wait_send()
        for q in range(quads):
            state_copy(q).wait_send()

    @pl.when(odd == 1)
    def _():
        @pl.when(ctx >= 2)
        def _():
            for q in range(quads):
                back_copy(q).wait_send()

        @pl.when(ctx < places_ctx - 2)
        def _():
            for q in range(quads):
                enter_copy(q).wait_send()


def per_device(
    places,
    hidden,
    norm_gain,
    zx_weight,
    bc_weight,
    dt_weight,
    conv_x,
    conv_bc,
    dt_bias,
    log_decay,
    skip_gain,
    out_gain,
    out_weight,
):
    rows, feat = hidden.shape
    width = zx_weight.shape[0]
    inner = zx_weight.shape[2]
    heads = dt_weight.shape[1]
    quads = inner // QUAD
    chunks = rows // BLOCK
    any_spec = pl.BlockSpec(memory_space=pl.ANY)
    vmem = pl.BlockSpec(memory_space=pltpu.VMEM)
    smem = pl.BlockSpec(memory_space=pltpu.SMEM)
    dma = pltpu.SemaphoreType.DMA
    return pl.pallas_call(
        functools.partial(kernel, places),
        out_shape=jax.ShapeDtypeStruct((rows, feat), BF16),
        in_specs=[any_spec] * 4 + [vmem] * 4 + [smem, vmem, smem, vmem],
        out_specs=vmem,
        scratch_shapes=[
            pltpu.VMEM((4, HALO + rows, feat), BF16),
            pltpu.VMEM((width, 2, inner), BF16),
            pltpu.VMEM((width, 2 * inner), BF16),
            pltpu.VMEM((width, 2 * STATE), BF16),
            pltpu.VMEM((inner, width), BF16),
            pltpu.VMEM((width, 128), BF16),
            pltpu.VMEM((8, 128), F32),
            pltpu.VMEM((8, inner), F32),
            pltpu.VMEM((BLOCK, width), BF16),
            pltpu.VMEM((HALO, inner + 2 * STATE), F32),
            pltpu.VMEM((128, BLOCK), F32),
            pltpu.VMEM((rows, inner), BF16),
            pltpu.VMEM((rows, inner), BF16),
            pltpu.VMEM((rows, STATE), BF16),
            pltpu.VMEM((rows, inner), F32),
            pltpu.VMEM((chunks, STATE, inner), BF16),
            pltpu.VMEM((chunks, 8, inner), F32),
            pltpu.VMEM((rows, 128), F32),
            pltpu.VMEM((STATE, inner), F32),
            pltpu.VMEM((8, inner), F32),
            pltpu.VMEM((quads, STATE, QUAD), BF16),
            pltpu.VMEM((8, inner), F32),
            pltpu.VMEM((quads, STATE, QUAD), BF16),
            pltpu.VMEM((8, inner), F32),
            pltpu.VMEM((quads, STATE, QUAD), BF16),
            pltpu.VMEM((quads, STATE, QUAD), BF16),
            pltpu.VMEM((quads, STATE, QUAD), BF16),
            pltpu.VMEM((STATE, inner), F32),
            pltpu.VMEM((BLOCK, inner), BF16),
            pltpu.VMEM((chunks, 2, BLOCK, feat), BF16),
            pltpu.VMEM((chunks, 2, BLOCK, feat), BF16),
            pltpu.VMEM((chunks, 2, BLOCK, feat), F32),
            pltpu.VMEM((chunks, BLOCK, feat), BF16),
            pltpu.VMEM((chunks, BLOCK, feat), BF16),
            pltpu.VMEM((4, chunks, 8, BLOCK), F32),
            dma((4,)),
            dma((chunks,)),
            dma((chunks,)),
            dma((chunks,)),
            dma((chunks,)),
            dma((chunks,)),
            dma((chunks,)),
            dma((4,)),
            dma((4,)),
            dma((quads + 1,)),
            dma((quads + 1,)),
            dma((quads,)),
            dma((quads,)),
            dma((quads,)),
            dma((quads,)),
            dma((chunks,)),
            dma((chunks,)),
            dma((chunks,)),
            dma((chunks,)),
            dma((3, chunks)),
            dma((3, chunks)),
        ],
        compiler_params=pltpu.CompilerParams(
            collective_id=0, has_side_effects=True, vmem_limit_bytes=63000000
        ),
        name="mixer",
    )(
        hidden,
        zx_weight,
        bc_weight,
        out_weight,
        norm_gain,
        dt_weight.T,
        conv_x,
        conv_bc,
        dt_bias,
        log_decay.T,
        skip_gain,
        out_gain,
    )


def solution(mesh):
    placed = (
        P("ctx", "head"),
        P(),
        P(None, None, "head"),
        P(),
        P(None, "head"),
        P(None, "head"),
        P(),
        P("head"),
        P("ctx", "head"),
        P("head"),
        P("head"),
        P("head", None),
    )
    return jax.shard_map(
        functools.partial(per_device, mesh.shape["ctx"]),
        mesh=mesh,
        in_specs=placed,
        out_specs=P("ctx", "head"),
        check_vma=False,
    )
```

```python
import functools

import jax
import jax.numpy as jnp
from jax import lax
from jax.experimental import pallas as pl
from jax.experimental.pallas import tpu as pltpu
from jax.sharding import PartitionSpec as P

HEADDIM = 64
STATE = 128
CONV = 4
BLOCK = 256
HALO = 16
QUAD = 256
GROUP = 128
PER = QUAD // HEADDIM

eps = 1e-05
F32 = jnp.float32
BF16 = jnp.bfloat16


def dot(a, b):
    return jnp.dot(a, b, preferred_element_type=F32)


def silu(v):
    return v / (1.0 + jnp.exp(-v))


def spread(column_of, first, lane, rows):
    out = None
    for k in range(PER):
        piece = jnp.broadcast_to(column_of(first + k), (rows, QUAD))
        out = piece if out is None else jnp.where(lane >= k * HEADDIM, piece, out)
    return out


def kernel(
    places,
    hidden,
    wzx_hbm,
    wbc_hbm,
    wout_hbm,
    gain,
    wdt_in,
    taps_x,
    taps_bc,
    dtb,
    ld_in,
    skip,
    out_gain,
    out,
    xg,
    wraw,
    wzx,
    wbc,
    wout,
    wdt,
    dtrow,
    skrow,
    nrm,
    tail,
    ldp,
    gate,
    xc,
    cm,
    yi,
    ent,
    tl,
    ed,
    st,
    dsum,
    got_s,
    got_d,
    snd_s,
    snd_d,
    got_e,
    snd_e,
    snd_b,
    back,
    inc,
    sc_keep,
    dc_keep,
    dr_keep,
    sr_keep,
    gb,
    send_p,
    recv_p,
    own,
    send_y,
    recv_y,
    sq,
    load_sem,
    ys,
    yr,
    ps,
    pr,
    fs,
    fr,
    hs,
    hr,
    cs,
    cr,
    es,
    er,
    bs,
    br,
    rs,
    rr,
    zs,
    zr,
    qs,
    qr,
):
    places_ctx = places
    rows, feat = hidden.shape
    width = 4 * feat
    inner = wzx.shape[1] // 2
    heads = inner // HEADDIM
    quads = inner // QUAD
    chunks = rows // BLOCK
    ctx = lax.axis_index("ctx")
    me = lax.axis_index("head")
    partner = me + 1 - 2 * lax.rem(me, 2)
    other = lax.rem(me + 2, 4)
    diag = lax.rem(partner + 2, 4)
    odd = lax.rem(ctx, 2)
    MESH = pl.DeviceIdType.MESH

    def remote(src, dst, ss, rsem, c, h):
        return pltpu.make_async_remote_copy(
            src_ref=src, dst_ref=dst, send_sem=ss, recv_sem=rsem, device_id=(c, h), device_id_type=MESH
        )

    own_load = pltpu.make_async_copy(hidden, xg.at[me, pl.ds(HALO, rows)], load_sem.at[0])
    loads = [
        pltpu.make_async_copy(wbc_hbm, wbc, load_sem.at[1]),
        pltpu.make_async_copy(wzx_hbm, wraw, load_sem.at[2]),
    ]
    out_load = pltpu.make_async_copy(wout_hbm, wout, load_sem.at[3])

    barrier = pltpu.get_barrier_semaphore()

    def greet(c, h):
        pl.semaphore_signal(barrier, inc=1, device_id=(c, h), device_id_type=MESH)

    for h in (partner, other, diag):
        greet(ctx, h)

    @pl.when(ctx > 0)
    def _():
        for h in range(4):
            greet(ctx - 1, h)

    @pl.when(ctx < places_ctx - 1)
    def _():
        for h in range(4):
            greet(ctx + 1, h)

    @pl.when(ctx >= 2)
    def _():
        greet(ctx - 2, me)

    @pl.when(ctx < places_ctx - 2)
    def _():
        greet(ctx + 2, me)

    own_load.start()
    for load in loads:
        load.start()
    out_load.start()
    below = lax.div(ctx + places_ctx - 1, places_ctx)
    above = lax.div(2 * places_ctx - 2 - ctx, places_ctx)
    two_below = lax.div(ctx + places_ctx - 2, places_ctx)
    two_above = lax.div(2 * places_ctx - 3 - ctx, places_ctx)
    pl.semaphore_wait(barrier, 3 + 4 * (below + above) + two_below + two_above)

    def src_rows(c):
        return hidden.at[pl.ds(pl.multiple_of(c * BLOCK, BLOCK), BLOCK)]

    def slot(h, c):
        return xg.at[h, pl.ds(pl.multiple_of(HALO + c * BLOCK, HALO), BLOCK)]

    def to_y(c):
        return remote(src_rows(c), slot(me, c), ys.at[c], yr.at[c], ctx, other)

    def to_p(c):
        return remote(src_rows(c), slot(me, c), ps.at[c], pr.at[c], ctx, partner)

    def forward(c):
        return remote(slot(other, c), slot(other, c), fs.at[c], fr.at[c], ctx, partner)

    def halo(h, sender):
        return remote(
            hidden.at[pl.ds(rows - HALO, HALO)],
            xg.at[sender, pl.ds(0, HALO)],
            hs.at[h],
            hr.at[sender],
            ctx + 1,
            h,
        )

    @pl.when(ctx < places_ctx - 1)
    def _():
        for h in range(4):
            halo(h, me).start()

    for c in range(chunks):
        to_y(c).start()
    for c in range(chunks):
        to_p(c).start()

    @pl.when(ctx == 0)
    def _():
        xg[:, 0:HALO, :] = jnp.zeros((4, HALO, feat), BF16)

    dt_wide = jnp.concatenate(
        [wdt_in[...].astype(F32), jnp.zeros((128 - heads, width), F32)], axis=0
    )
    wdt[...] = dt_wide.T.astype(BF16)
    few = lax.broadcasted_iota(jnp.int32, (8, 128), 1)
    bias_row = jnp.zeros((8, 128), F32)
    for h in range(heads):
        bias_row = jnp.where(few == h, dtb[h], bias_row)
    dtrow[...] = bias_row
    wide = lax.broadcasted_iota(jnp.int32, (8, inner), 1)
    skip_row = jnp.zeros((8, inner), F32)
    for h in range(heads):
        skip_row = jnp.where(wide >= h * HEADDIM, skip[h], skip_row)
    skrow[...] = skip_row
    ldp[...] = jnp.zeros_like(ldp)
    st[...] = jnp.zeros_like(st)
    dsum[...] = jnp.zeros_like(dsum)

    @pl.when(ctx > 0)
    def _():
        for h in range(4):
            halo(0, h).wait_recv()

    for load in loads:
        load.wait()
    own_load.wait()

    def split(i, carry):
        at = pl.ds(pl.multiple_of(i * 64, 64), 64)
        both = wraw[at, :, :]
        wzx[at, 0:inner] = both[:, 0, :]
        wzx[at, inner : 2 * inner] = both[:, 1, :]
        return carry

    lax.fori_loop(0, width // 64, split, 0)

    def normalised(at, count):
        vals = [xg[j, at, :].astype(F32) for j in range(4)]
        total = sum(jnp.sum(v * v, axis=-1, keepdims=True) for v in vals)
        scale = lax.rsqrt(total / width + eps)
        for j in range(4):
            span = slice(j * feat, (j + 1) * feat)
            nrm[0:count, span] = (vals[j] * scale * gain[span].reshape(1, feat)).astype(BF16)

    normalised(pl.ds(0, HALO), HALO)
    head_rows = nrm[0:HALO, :]
    for s in range(quads):
        tail[:, s * QUAD : (s + 1) * QUAD] = dot(
            head_rows, wzx[:, inner + s * QUAD : inner + (s + 1) * QUAD]
        )
    tail[:, inner : inner + 2 * STATE] = dot(head_rows, wbc[...])

    lane = lax.broadcasted_iota(jnp.int32, (1, QUAD), 1)
    row_id = lax.broadcasted_iota(jnp.int32, (BLOCK, BLOCK), 0)
    col_id = lax.broadcasted_iota(jnp.int32, (BLOCK, BLOCK), 1)

    def convolved(raw, span, taps):
        ext = jnp.concatenate([tail[:, span], raw], axis=0)
        summed = taps[CONV : CONV + 1, :] + taps[CONV - 1 : CONV, :] * ext
        for back_by in range(1, CONV):
            at = CONV - 1 - back_by
            summed = summed + taps[at : at + 1, :] * pltpu.roll(ext, back_by, 0)
        tail[:, span] = raw[BLOCK - HALO :, :]
        return silu(summed[HALO:, :])

    def inside(c):
        here = pl.ds(pl.multiple_of(c * BLOCK, BLOCK), BLOCK)
        scores = sc_keep[...]
        for q in range(quads):
            span = slice(q * QUAD, (q + 1) * QUAD)
            xq = xc[here, span]
            y_acc = None
            for k in range(PER):
                h = q * PER + k
                gap = jnp.minimum(dc_keep[:, h : h + 1] - dr_keep[h : h + 1, :], 0.0)
                mix = (scores * jnp.exp(gap) * sr_keep[h : h + 1, :]).astype(BF16)
                y_h = dot(mix, xq)
                y_acc = y_h if k == 0 else jnp.where(lane >= k * HEADDIM, y_h, y_acc)
            yi[here, span] = y_acc

    def first(c, carry):
        @pl.when(c > 0)
        def _():
            inside(c - 1)

        to_y(c).wait_recv()
        forward(c).start()
        to_p(c).wait_recv()
        remote(slot(diag, c), slot(diag, c), fs.at[c], fr.at[c], ctx, partner).wait_recv()
        here = pl.ds(pl.multiple_of(c * BLOCK, BLOCK), BLOCK)
        normalised(pl.ds(pl.multiple_of(HALO + c * BLOCK, HALO), BLOCK), BLOCK)
        normed = nrm[...]
        bc = convolved(dot(normed, wbc[...]), slice(inner, inner + 2 * STATE), taps_bc[...])
        b = bc[:, :STATE].astype(BF16)
        cc = bc[:, STATE:].astype(BF16)
        cm[here, :] = cc
        raw_step = dot(normed, wdt[...]) + dtrow[0:1, :]
        step = jnp.maximum(raw_step, 0.0) + jnp.log1p(jnp.exp(-jnp.abs(raw_step)))
        ldp[0:heads, :] = ld_in[:, here]
        tri = jnp.where(row_id <= col_id, 1.0, 0.0).astype(F32)
        drow = jnp.dot(ldp[...], tri, preferred_element_type=F32, precision=lax.Precision.HIGHEST)
        dcol = drow.T
        ed[here, :] = jnp.exp(dcol)
        srow = step.T
        wrow = jnp.exp(drow[:, BLOCK - 1 : BLOCK] - drow) * srow
        scores = lax.dot_general(
            cc, b, (((1,), (1,)), ((), ())), preferred_element_type=F32
        )
        sc_keep[...] = jnp.where(row_id >= col_id, scores, 0.0)
        dc_keep[...] = dcol
        dr_keep[...] = drow[0:16, :]
        sr_keep[...] = srow[0:16, :]
        b_t = b.astype(F32).T
        for q in range(quads):
            span = slice(q * QUAD, (q + 1) * QUAD)
            gate[here, span] = dot(normed, wzx[:, span]).astype(BF16)
            raw = dot(normed, wzx[:, inner + q * QUAD : inner + (q + 1) * QUAD])
            xq = convolved(raw, span, taps_x[:, span]).astype(BF16)
            xc[here, span] = xq
            s_acc = None
            for k in range(PER):
                h = q * PER + k
                wb = (b_t * wrow[h : h + 1, :]).astype(BF16)
                s_h = dot(wb, xq)
                if k == 0:
                    s_acc = s_h
                else:
                    s_acc = jnp.where(lane >= k * HEADDIM, s_h, s_acc)
            total = spread(lambda i: dcol[BLOCK - 1 : BLOCK, i : i + 1], q * PER, lane, 1)
            ent[c, :, span] = st[:, span].astype(BF16)
            tl[c, :, span] = dsum[:, span]
            st[:, span] = jnp.exp(total) * st[:, span] + s_acc
            dsum[:, span] = dsum[:, span] + total
        return carry

    lax.fori_loop(0, chunks, first, 0)

    groups = inner // GROUP

    def part(g):
        return slice(g * GROUP, (g + 1) * GROUP)

    def state_copy(g, c):
        return remote(snd_s.at[g], got_s.at[g], cs.at[g], cr.at[g], c, me)

    def decay_copy(c):
        return remote(snd_d, got_d, cs.at[groups], cr.at[groups], c, me)

    def enter_copy(g):
        return remote(snd_e.at[g], got_e.at[g], es.at[g], er.at[g], ctx + 2, me)

    def back_copy(g, c):
        return remote(snd_b.at[g], back.at[g], bs.at[g], br.at[g], c, me)

    even_led = [g for g in range(groups) if g % 2 == 0]
    odd_led = [g for g in range(groups) if g % 2 == 1]

    def pair_scan(is_odd, mate, led, followed):
        snd_d[...] = dsum[...]
        decay_copy(mate).start()
        for g in followed:
            snd_s[g] = st[:, part(g)].astype(BF16)
            state_copy(g, mate).start()
        inside(chunks - 1)
        decay_copy(mate).wait_recv()
        for g in led:
            at = part(g)
            state_copy(g, mate).wait_recv()
            mine = dsum[0:1, at]
            theirs = got_d[0:1, at]
            if is_odd:
                pair = jnp.exp(mine) * got_s[g].astype(F32) + st[:, at]
            else:
                pair = jnp.exp(theirs) * st[:, at] + got_s[g].astype(F32)

            @pl.when(ctx >= 2)
            def _():
                enter_copy(g).wait_recv()

            entered = got_e[g].astype(F32)

            @pl.when(ctx < places_ctx - 2)
            def _():
                snd_e[g] = (jnp.exp(mine + theirs) * entered + pair).astype(BF16)
                enter_copy(g).start()

            if is_odd:
                snd_b[g] = got_e[g]
                inc[:, at] = jnp.exp(theirs) * entered + got_s[g].astype(F32)
            else:
                snd_b[g] = (jnp.exp(mine) * entered + st[:, at]).astype(BF16)
                inc[:, at] = entered
            back_copy(g, mate).start()
        for g in followed:
            back_copy(g, mate).wait_recv()
            inc[:, part(g)] = back[g].astype(F32)
        decay_copy(mate).wait_send()
        for g in followed:
            state_copy(g, mate).wait_send()
        for g in led:
            back_copy(g, mate).wait_send()

        @pl.when(ctx < places_ctx - 2)
        def _():
            for g in led:
                enter_copy(g).wait_send()

    @pl.when(ctx < 2)
    def _():
        got_e[...] = jnp.zeros_like(got_e)

    @pl.when(odd == 0)
    def _():
        pair_scan(0, ctx + 1, even_led, odd_led)

    @pl.when(odd == 1)
    def _():
        pair_scan(1, ctx - 1, odd_led, even_led)

    out_load.wait()

    def piece_copy(c):
        return remote(send_p.at[c], recv_p.at[c], rs.at[c], rr.at[c], ctx, partner)

    def far_copy(c):
        return remote(send_y.at[c], recv_y.at[c], zs.at[c], zr.at[c], ctx, other)

    def square_copy(c, h, k, sender):
        return remote(sq.at[sender, c], sq.at[sender, c], qs.at[k, c], qr.at[k, c], ctx, h)

    def columns(h):
        return pl.ds(pl.multiple_of(h * feat, 128), feat)

    def combine(c):
        piece_copy(c).wait_recv()
        own[c, 0] = own[c, 0] + recv_p[c, 0].astype(F32)
        send_y[c] = (own[c, 1] + recv_p[c, 1].astype(F32)).astype(BF16)
        far_copy(c).start()

    def second(c, carry):
        here = pl.ds(pl.multiple_of(c * BLOCK, BLOCK), BLOCK)
        squares = jnp.zeros((BLOCK, 1), F32)
        e_all = ed[here, :]
        cc = cm[here, :]
        for q in range(quads):
            span = slice(q * QUAD, (q + 1) * QUAD)
            carried = ent[c, :, span].astype(F32) + jnp.exp(tl[c, 0:1, span]) * inc[:, span]
            yc = dot(cc, carried.astype(BF16))
            growth = spread(lambda i: e_all[:, i : i + 1], q * PER, lane, BLOCK)
            y = yi[here, span] + growth * yc + skrow[0:1, span] * xc[here, span].astype(F32)
            gated = y * silu(gate[here, span].astype(F32))
            squares = squares + jnp.sum(gated * gated, axis=-1, keepdims=True)
            gb[:, span] = (gated * out_gain[span].reshape(1, QUAD)).astype(BF16)
        g = gb[...]
        send_p[c, 0] = dot(g, wout[:, columns(partner)]).astype(BF16)
        send_p[c, 1] = dot(g, wout[:, columns(diag)]).astype(BF16)
        piece_copy(c).start()
        sq[me, c] = jnp.broadcast_to(squares, (BLOCK, 128)).T[0:8, :]
        for k, h in enumerate((partner, other, diag)):
            square_copy(c, h, k, me).start()
        own[c, 1] = dot(g, wout[:, columns(other)])
        own[c, 0] = dot(g, wout[:, columns(me)])

        @pl.when(c > 0)
        def _():
            combine(c - 1)

        return carry

    lax.fori_loop(0, chunks, second, 0)
    combine(chunks - 1)

    def third(c, carry):
        here = pl.ds(pl.multiple_of(c * BLOCK, BLOCK), BLOCK)
        for k, h in enumerate((partner, other, diag)):
            square_copy(c, h, k, h).wait_recv()
        total = (sq[0, c] + sq[1, c]) + (sq[2, c] + sq[3, c])
        scale_row = lax.rsqrt(total / (4 * inner) + eps)
        scale = jnp.broadcast_to(scale_row[0:1, :], (128, BLOCK)).T[:, 0:1]
        far_copy(c).wait_recv()
        out[here, :] = ((own[c, 0] + recv_y[c].astype(F32)) * scale).astype(BF16)
        return carry

    lax.fori_loop(0, chunks, third, 0)

    for c in range(chunks):
        to_y(c).wait_send()
        to_p(c).wait_send()
        forward(c).wait_send()
        piece_copy(c).wait_send()
        far_copy(c).wait_send()
        for k, h in enumerate((partner, other, diag)):
            square_copy(c, h, k, me).wait_send()

    @pl.when(ctx < places_ctx - 1)
    def _():
        for h in range(4):
            halo(h, me).wait_send()


def per_device(
    places,
    hidden,
    norm_gain,
    zx_weight,
    bc_weight,
    dt_weight,
    conv_x,
    conv_bc,
    dt_bias,
    log_decay,
    skip_gain,
    out_gain,
    out_weight,
):
    rows, feat = hidden.shape
    width = zx_weight.shape[0]
    inner = zx_weight.shape[2]
    heads = dt_weight.shape[1]
    groups = inner // GROUP
    chunks = rows // BLOCK
    any_spec = pl.BlockSpec(memory_space=pl.ANY)
    vmem = pl.BlockSpec(memory_space=pltpu.VMEM)
    smem = pl.BlockSpec(memory_space=pltpu.SMEM)
    dma = pltpu.SemaphoreType.DMA
    return pl.pallas_call(
        functools.partial(kernel, places),
        out_shape=jax.ShapeDtypeStruct((rows, feat), BF16),
        in_specs=[any_spec] * 4 + [vmem] * 4 + [smem, vmem, smem, vmem],
        out_specs=vmem,
        scratch_shapes=[
            pltpu.VMEM((4, HALO + rows, feat), BF16),
            pltpu.VMEM((width, 2, inner), BF16),
            pltpu.VMEM((width, 2 * inner), BF16),
            pltpu.VMEM((width, 2 * STATE), BF16),
            pltpu.VMEM((inner, width), BF16),
            pltpu.VMEM((width, 128), BF16),
            pltpu.VMEM((8, 128), F32),
            pltpu.VMEM((8, inner), F32),
            pltpu.VMEM((BLOCK, width), BF16),
            pltpu.VMEM((HALO, inner + 2 * STATE), F32),
            pltpu.VMEM((128, BLOCK), F32),
            pltpu.VMEM((rows, inner), BF16),
            pltpu.VMEM((rows, inner), BF16),
            pltpu.VMEM((rows, STATE), BF16),
            pltpu.VMEM((rows, inner), F32),
            pltpu.VMEM((chunks, STATE, inner), BF16),
            pltpu.VMEM((chunks, 8, inner), F32),
            pltpu.VMEM((rows, 128), F32),
            pltpu.VMEM((STATE, inner), F32),
            pltpu.VMEM((8, inner), F32),
            pltpu.VMEM((groups, STATE, GROUP), BF16),
            pltpu.VMEM((8, inner), F32),
            pltpu.VMEM((groups, STATE, GROUP), BF16),
            pltpu.VMEM((8, inner), F32),
            pltpu.VMEM((groups, STATE, GROUP), BF16),
            pltpu.VMEM((groups, STATE, GROUP), BF16),
            pltpu.VMEM((groups, STATE, GROUP), BF16),
            pltpu.VMEM((groups, STATE, GROUP), BF16),
            pltpu.VMEM((STATE, inner), F32),
            pltpu.VMEM((BLOCK, BLOCK), F32),
            pltpu.VMEM((BLOCK, 128), F32),
            pltpu.VMEM((16, BLOCK), F32),
            pltpu.VMEM((16, BLOCK), F32),
            pltpu.VMEM((BLOCK, inner), BF16),
            pltpu.VMEM((chunks, 2, BLOCK, feat), BF16),
            pltpu.VMEM((chunks, 2, BLOCK, feat), BF16),
            pltpu.VMEM((chunks, 2, BLOCK, feat), F32),
            pltpu.VMEM((chunks, BLOCK, feat), BF16),
            pltpu.VMEM((chunks, BLOCK, feat), BF16),
            pltpu.VMEM((4, chunks, 8, BLOCK), F32),
            dma((4,)),
            dma((chunks,)),
            dma((chunks,)),
            dma((chunks,)),
            dma((chunks,)),
            dma((chunks,)),
            dma((chunks,)),
            dma((4,)),
            dma((4,)),
            dma((groups + 1,)),
            dma((groups + 1,)),
            dma((groups,)),
            dma((groups,)),
            dma((groups,)),
            dma((groups,)),
            dma((chunks,)),
            dma((chunks,)),
            dma((chunks,)),
            dma((chunks,)),
            dma((3, chunks)),
            dma((3, chunks)),
        ],
        compiler_params=pltpu.CompilerParams(
            collective_id=0, has_side_effects=True, vmem_limit_bytes=63000000
        ),
        name="mixer",
    )(
        hidden,
        zx_weight,
        bc_weight,
        out_weight,
        norm_gain,
        dt_weight.T,
        conv_x,
        conv_bc,
        dt_bias,
        log_decay.T,
        skip_gain,
        out_gain,
    )


def solution(mesh):
    placed = (
        P("ctx", "head"),
        P(),
        P(None, None, "head"),
        P(),
        P(None, "head"),
        P(None, "head"),
        P(),
        P("head"),
        P("ctx", "head"),
        P("head"),
        P("head"),
        P("head", None),
    )
    return jax.shard_map(
        functools.partial(per_device, mesh.shape["ctx"]),
        mesh=mesh,
        in_specs=placed,
        out_specs=P("ctx", "head"),
        check_vma=False,
    )
```
